512 devices in a mesh: row: 256 (over z, y, x), col: 2 (over core).
Axes of the slice: x: 4, y: 8, z: 8, core: 2. Of those that a mesh axis runs over, the one named last changes fastest.
Arguments:
- panel: bfloat16 [262144, 4096], P('row', 'col'), may hold values from -60 to 60, as said below
- sketch: bfloat16 [4096, 256], P('col'), may hold values from -0.09375 to 0.09375
Outputs:
- basis: float32 [262144, 256], P(('row', 'col'))
- upper: float32 [256, 256], replicated
The draws below stay inside these ranges and needn't reach their ends.
Inputs may be any that keep to these rules, and one draw needn't show every extreme that they name: `panel`: scaled expression values, real-valued, with scales that differ from cell to cell and from gene to gene.
All inputs are finite; a program needn't handle non-finite values.
Results may differ from the reference program's by a relative error of at most 0.0003.
Values sent between devices are 32-bit elements; how exact they have to be, the bound alone decides.
No kernel may reach another device: no remote copies, remote signals or barrier semaphores. Data moves between devices by JAX's collectives and lax.ppermute only.
A program may use at most 64 MiB of HBM per device.

```python
import jax
import jax.numpy as jnp
from jax import lax

GP = 4096
S = 256
NROWS = 262144


def draw_panel(key, part):
    keys = jax.random.split(key, 3)
    values = jax.random.normal(keys[0], (NROWS, GP), jnp.float32)
    ramp = jnp.exp(jnp.log(3.0) * jnp.arange(NROWS, dtype=jnp.float32) / NROWS)
    row_scale = jnp.exp(jnp.log(10.0) * jax.random.uniform(keys[1], (NROWS, 1), jnp.float32)) * ramp[:, None] / 10.0
    col_scale = jnp.exp(jnp.log(10.0) * jax.random.uniform(keys[2], (1, GP), jnp.float32)) / 3.16
    return jnp.clip(values * row_scale * col_scale, -60.0, 60.0).astype(jnp.bfloat16)


def levels(stream_key, extent, cuts, low, high):
    level, own = 1.0, jax.random.fold_in(stream_key, 6)
    for axis_at, blocks in cuts:
        draws = jnp.exp(jax.random.uniform(jax.random.fold_in(own, axis_at), (blocks,), jnp.float32, low / len(cuts), high / len(cuts)))
        level = level * jnp.repeat(draws, extent[axis_at] // blocks).reshape([-1 if axis == axis_at else 1 for axis in range(len(extent))])
    return level


def gaussian(rng, shape, width, bound, shards=(), kind=jnp.bfloat16):
    values = width * jax.random.normal(rng, shape, jnp.float32)
    if shards:
        values = values * levels(rng, shape, shards, -0.22, 0.18)
    return jnp.clip(values, -bound, bound).astype(kind)


def setup_inputs(seed: int = 0) -> dict:
    streams_of = jax.random.split(jax.random.key(seed), 3)
    panel = draw_panel(jax.random.fold_in(streams_of[2], 71), 0)
    sketch = gaussian(streams_of[1], (GP, S), GP ** -0.5, 0.09375, ((0, 2),))
    return {"panel": panel, "sketch": sketch}


def reference(panel, sketch):
    sampled = jnp.dot(panel.astype(jnp.float32), sketch.astype(jnp.float32), preferred_element_type=jnp.float32)
    gram = jnp.dot(sampled.T, sampled, precision=lax.Precision.HIGHEST) / NROWS
    upper = jnp.linalg.cholesky(gram).T
    basis = jax.scipy.linalg.solve_triangular(upper.T, sampled.T, lower=True).T
    return (basis, upper)
```

```python
import functools

import jax
import jax.numpy as jnp
from jax import lax
from jax.experimental import pallas as pl
from jax.experimental.pallas import tpu as pltpu
from jax.sharding import Mesh
from jax.sharding import PartitionSpec as P

ROW = ("z", "y", "x")
ROW_COL = ("z", "y", "x", "col")
SCATTER = ("z", "x")
SHARED = ("y", "col")
F32 = jnp.float32
HIGHEST = lax.Precision.HIGHEST
VMEM = pl.BlockSpec(memory_space=pltpu.VMEM)
HALF = 128
PACKED = 288
SMALL = pltpu.CompilerParams(vmem_limit_bytes=12 << 20)
LARGE = pltpu.CompilerParams(vmem_limit_bytes=63_500_288)


def dot(a, b, dim_a, dim_b):
    dims = (((dim_a,), (dim_b,)), ((), ()))
    return lax.dot_general(a, b, dims, precision=HIGHEST, preferred_element_type=F32)


def product_kernel(which_ref, panel_ref, sketch_ref, out_ref):
    out_ref[...] = jnp.dot(panel_ref[...], sketch_ref[...], preferred_element_type=F32)


def product(which, panel, sketch):
    rows, depth = panel.shape
    columns = sketch.shape[1]
    half, tile = rows // 2, 128
    steps = half // tile
    return pl.pallas_call(
        product_kernel,
        out_shape=jax.ShapeDtypeStruct((half, columns), F32),
        grid_spec=pltpu.PrefetchScalarGridSpec(
            num_scalar_prefetch=1,
            grid=(steps,),
            in_specs=[
                pl.BlockSpec((tile, depth), lambda i, which: (which[0] * steps + i, 0)),
                pl.BlockSpec((depth, columns), lambda i, which: (0, 0)),
            ],
            out_specs=pl.BlockSpec((tile, columns), lambda i, which: (i, 0)),
        ),
        cost_estimate=pl.CostEstimate(
            flops=2 * half * depth * columns,
            bytes_accessed=2 * (half + columns) * depth + 4 * half * columns,
            transcendentals=0,
        ),
        compiler_params=LARGE,
        name="product",
    )(which, panel, sketch)


def gram_kernel(own_ref, came_ref, block_ref, packed_ref):
    whole = own_ref[...] + came_ref[...]
    block_ref[...] = whole
    left, right = whole[:, :HALF], whole[:, HALF:]
    first = dot(left, left, 0, 0)
    packed_ref[HALF : 2 * HALF, :] = dot(left, right, 0, 0)
    last = dot(right, right, 0, 0)
    row = lax.broadcasted_iota(jnp.int32, (HALF, HALF), 0)
    lane = lax.broadcasted_iota(jnp.int32, (HALF, HALF), 1)
    packed_ref[:HALF, :] = jnp.where(lane >= row, first, last)
    diagonal = jnp.sum(jnp.where(lane == row, last, 0.0), axis=0, keepdims=True)
    packed_ref[2 * HALF :, :] = jnp.broadcast_to(diagonal, (PACKED - 2 * HALF, HALF))


def gram_of(own, came):
    return pl.pallas_call(
        gram_kernel,
        out_shape=(
            jax.ShapeDtypeStruct(own.shape, F32),
            jax.ShapeDtypeStruct((PACKED, HALF), F32),
        ),
        in_specs=[VMEM] * 2,
        out_specs=(VMEM, VMEM),
        compiler_params=SMALL,
        name="gram",
    )(own, came)


def sub(x, j):
    return jnp.broadcast_to(x[j : j + 1, :], (8, HALF))


def lane_of(x, j):
    return jnp.broadcast_to(x[:, j : j + 1], (8, HALF))


def eliminate(rows, extra):
    count = len(rows)
    rows, extra = list(rows), [list(e) for e in extra]
    sublane = lax.broadcasted_iota(jnp.int32, (8, HALF), 0)
    for g in range(count):
        c = [lane_of(rows[g], 8 * g + m) for m in range(8)]
        inverses, units, pivots = [], [], None
        for j in range(8):
            pivot = sub(c[j], j)
            pivots = pivot if j == 0 else jnp.where(sublane == j, pivot, pivots)
            inverse = 1.0 / pivot
            unit = c[j] * inverse
            for m in range(j + 1, 8):
                c[m] = c[m] - unit * sub(c[j], m)
            inverses.append(inverse)
            units.append(unit)
        parts = [rows[g]] + extra[g]
        for j in range(7):
            below = jnp.where(sublane > j, units[j], 0.0)
            parts = [x - below * sub(x, j) for x in parts]
        spread = [[sub(x, j) for x in parts] for j in range(8)]
        for h in range(g + 1, count):
            d = [lane_of(rows[h], 8 * g + m) for m in range(8)]
            lower = [rows[h]] + extra[h]
            for j in range(8):
                unit = d[j] * inverses[j]
                for m in range(j + 1, 8):
                    d[m] = d[m] - unit * sub(c[j], m)
                lower = [x - unit * b for x, b in zip(lower, spread[j])]
            rows[h], extra[h] = lower[0], lower[1:]
        scale = lax.rsqrt(pivots)
        parts = [x * scale for x in parts]
        rows[g], extra[g] = parts[0], parts[1:]
    return rows, extra


def factor_kernel(total_rows, packed_ref, block_ref, basis_ref, upper_ref, a11, a22, inv1, u12, inv2):
    row = lax.broadcasted_iota(jnp.int32, (HALF, HALF), 0)
    lane = lax.broadcasted_iota(jnp.int32, (HALF, HALF), 1)
    mixed = packed_ref[:HALF, :] / total_rows
    turned = mixed.T
    diagonal = packed_ref[2 * HALF : 2 * HALF + 1, :] / total_rows
    a11[...] = jnp.where(lane >= row, mixed, turned)
    a22[...] = jnp.where(lane == row, diagonal, jnp.where(lane < row, mixed, turned))
    sublane8 = lax.broadcasted_iota(jnp.int32, (8, HALF), 0)
    lane8 = lax.broadcasted_iota(jnp.int32, (8, HALF), 1)
    groups = [slice(8 * k, 8 * k + 8) for k in range(HALF // 8)]
    eye = [jnp.where(lane8 == sublane8 + 8 * k, 1.0, 0.0) for k in range(HALF // 8)]

    def kept(x, k):
        return jnp.where(lane8 >= sublane8 + 8 * k, x, 0.0)

    rows = [a11[at, :] for at in groups]
    extra = [
        [packed_ref[HALF + 8 * k : HALF + 8 * k + 8, :] / total_rows, eye[k]]
        for k in range(len(groups))
    ]
    rows, extra = eliminate(rows, extra)
    for k, at in enumerate(groups):
        upper_ref[at, :HALF] = kept(rows[k], k)
        upper_ref[at, HALF:] = extra[k][0]
        upper_ref[HALF + 8 * k : HALF + 8 * k + 8, :HALF] = jnp.zeros((8, HALF), F32)
        u12[at, :] = extra[k][0]
        inv1[at, :] = extra[k][1]
    across = u12[...]
    a22[...] = a22[...] - dot(across, across, 0, 0)
    first = dot(block_ref[:, :HALF], inv1[...], 1, 1)
    basis_ref[:, :HALF] = first
    rest = block_ref[:, HALF:] - dot(first, across, 1, 0)
    rows, extra = eliminate([a22[at, :] for at in groups], [[e] for e in eye])
    for k, at in enumerate(groups):
        upper_ref[HALF + 8 * k : HALF + 8 * k + 8, HALF:] = kept(rows[k], k)
        inv2[at, :] = extra[k][0]
    basis_ref[:, HALF:] = dot(rest, inv2[...], 1, 1)


def factor(total_rows, packed, block):
    return pl.pallas_call(
        functools.partial(factor_kernel, float(total_rows)),
        out_shape=(
            jax.ShapeDtypeStruct(block.shape, F32),
            jax.ShapeDtypeStruct((2 * HALF, 2 * HALF), F32),
        ),
        in_specs=[VMEM] * 2,
        out_specs=(VMEM, VMEM),
        scratch_shapes=[pltpu.VMEM((HALF, HALF), F32)] * 5,
        compiler_params=SMALL,
        name="factor",
    )(packed, block)


def exchanged(x, axis):
    return lax.all_to_all(x, axis, 0, 0, tiled=True)


def reduced(packed):
    owners, sharers = lax.axis_size(SCATTER), lax.axis_size(SHARED)
    pieces = packed.reshape(owners, 1, -1)
    mine = jnp.sum(exchanged(pieces, SCATTER), axis=0, keepdims=True)
    mine = jnp.broadcast_to(mine, (sharers, *mine.shape[1:]))
    mine = jnp.sum(exchanged(mine, SHARED), axis=0, keepdims=True)
    mine = jnp.broadcast_to(mine, (owners, *mine.shape[1:]))
    return exchanged(mine, SCATTER).reshape(packed.shape)


def local(panel, sketch):
    total_rows = panel.shape[0] * lax.axis_size(ROW)
    core = lax.axis_index("col").astype(jnp.int32).reshape(1)
    other = product(1 - core, panel, sketch)
    came = lax.ppermute(other, "col", [(0, 1), (1, 0)])
    own = product(core, panel, sketch)
    block, packed = gram_of(own, came)
    return factor(total_rows, reduced(packed), block)


def solution(mesh):
    sizes = (8, 8, 4, mesh.shape["col"])
    finer = Mesh(mesh.devices.reshape(sizes), ROW_COL)
    in_specs = (P(ROW, "col"), P("col", None))
    out_specs = (P(ROW_COL, None), P())
    return jax.shard_map(local, mesh=finer, in_specs=in_specs, out_specs=out_specs, check_vma=False)
```

```python
import functools

import jax
import jax.numpy as jnp
from jax import lax
from jax.experimental import pallas as pl
from jax.experimental.pallas import tpu as pltpu
from jax.sharding import Mesh
from jax.sharding import PartitionSpec as P

ROW = ("z_hi", "z_lo", "y_hi", "y_lo", "x")
ROW_COL = (*ROW, "col")
SCATTER = ("z_lo", "y_lo", "x", "col")
SHARED = ("z_hi", "y_hi")
F32 = jnp.float32
HIGHEST = lax.Precision.HIGHEST
VMEM = pl.BlockSpec(memory_space=pltpu.VMEM)
HBM = pl.BlockSpec(memory_space=pltpu.HBM)
HALF = 128
PACKED = 288
SMALL = pltpu.CompilerParams(vmem_limit_bytes=12 << 20)
CHUNKS = 4


def dot(a, b, dim_a, dim_b):
    dims = (((dim_a,), (dim_b,)), ((), ()))
    return lax.dot_general(a, b, dims, precision=HIGHEST, preferred_element_type=F32)


def product_kernel(which_ref, panel_ref, sketch_ref, out_ref, rows, table, sems):
    half = out_ref.shape[0]
    depth = table.shape[0]
    start = pl.multiple_of(which_ref[0] * half, half)
    width = depth // CHUNKS
    copies = []
    for k in range(CHUNKS):
        at = slice(k * width, (k + 1) * width)
        sources = (sketch_ref.at[at, :], panel_ref.at[pl.ds(start, half), at])
        for n, (source, target) in enumerate(zip(sources, (table.at[at, :], rows.at[:, at]))):
            copies.append(pltpu.make_async_copy(source, target, sems.at[n, k]))
            copies[-1].start()
    for k in range(CHUNKS):
        at = slice(k * width, (k + 1) * width)
        copies[2 * k].wait()
        copies[2 * k + 1].wait()
        part = jnp.dot(rows[:, at], table[at, :], preferred_element_type=F32)
        out_ref[...] = part if k == 0 else out_ref[...] + part


def in_hbm(x):
    return pltpu.with_memory_space_constraint(x, pltpu.HBM)


def product(which, panel, sketch):
    rows, depth = panel.shape
    columns = sketch.shape[1]
    half = rows // 2
    return pl.pallas_call(
        product_kernel,
        out_shape=jax.ShapeDtypeStruct((half, columns), F32),
        in_specs=[pl.BlockSpec(memory_space=pltpu.SMEM), HBM, HBM],
        out_specs=VMEM,
        scratch_shapes=[
            pltpu.VMEM((half, depth), panel.dtype),
            pltpu.VMEM((depth, columns), sketch.dtype),
            pltpu.SemaphoreType.DMA((2, CHUNKS)),
        ],
        cost_estimate=pl.CostEstimate(
            flops=2 * half * depth * columns,
            bytes_accessed=2 * (half + columns) * depth + 4 * half * columns,
            transcendentals=0,
        ),
        compiler_params=SMALL,
        name="product",
    )(which, in_hbm(panel), in_hbm(sketch))


def gram_kernel(own_ref, came_ref, block_ref, packed_ref):
    whole = own_ref[...] + came_ref[...]
    block_ref[...] = whole
    left, right = whole[:, :HALF], whole[:, HALF:]
    first = dot(left, left, 0, 0)
    packed_ref[HALF : 2 * HALF, :] = dot(left, right, 0, 0)
    last = dot(right, right, 0, 0)
    row = lax.broadcasted_iota(jnp.int32, (HALF, HALF), 0)
    lane = lax.broadcasted_iota(jnp.int32, (HALF, HALF), 1)
    packed_ref[:HALF, :] = jnp.where(lane >= row, first, last)
    diagonal = jnp.sum(jnp.where(lane == row, last, 0.0), axis=0, keepdims=True)
    packed_ref[2 * HALF :, :] = jnp.broadcast_to(diagonal, (PACKED - 2 * HALF, HALF))


def gram_of(own, came):
    return pl.pallas_call(
        gram_kernel,
        out_shape=(
            jax.ShapeDtypeStruct(own.shape, F32),
            jax.ShapeDtypeStruct((PACKED, HALF), F32),
        ),
        in_specs=[VMEM] * 2,
        out_specs=(VMEM, VMEM),
        compiler_params=SMALL,
        name="gram",
    )(own, came)


def sub(x, j):
    return jnp.broadcast_to(x[j : j + 1, :], (8, HALF))


def lane_of(x, j):
    return jnp.broadcast_to(x[:, j : j + 1], (8, HALF))


def eliminate(work):
    sublane = lax.broadcasted_iota(jnp.int32, (8, HALF), 0)
    size, width = work.shape
    tiles = [slice(t, t + HALF) for t in range(0, width, HALF)]
    block = 16
    for first in range(0, size, block):
        count = min(4, (size - first) // 8)
        rows = [[work[first + 8 * g : first + 8 * g + 8, t] for t in tiles] for g in range(count)]
        cols = [
            [lane_of(rows[g][0], first + m) for m in range(block)]
            for g in range(count)
        ]
        for g in range(2):
            cols[g][0] = jnp.where(sublane < 8, cols[g][0], 0.0)
        pivots = [None, None]
        for j in range(block):
            home, at = divmod(j, 8)
            pivot = sub(cols[home][j], at)
            pivots[home] = pivot if at == 0 else jnp.where(sublane == at, pivot, pivots[home])
            inverse = 1.0 / pivot
            units = [cols[g][j] * inverse for g in range(count)]
            for m in range(j + 1, block):
                spread = sub(cols[m // 8][j], m % 8)
                for g in range(home, count):
                    if g < 2 and m >= 8 * (g + 1):
                        continue
                    cols[g][m] = cols[g][m] - units[g] * spread
            units[home] = jnp.where(sublane > at, units[home], 0.0)
            for t in range(len(tiles)):
                spread = sub(rows[home][t], at)
                for g in range(home, count):
                    rows[g][t] = rows[g][t] - units[g] * spread
        for g in range(count):
            scale = lax.rsqrt(pivots[g]) if g < 2 else None
            for t, tile in enumerate(tiles):
                x = rows[g][t] if scale is None else rows[g][t] * scale
                work[first + 8 * g : first + 8 * g + 8, tile] = x
        far = first + 2 * block
        if far < size:
            done = work[first : first + block, :]
            change = dot(done[:, :HALF], done, 0, 0)
            work[far:, :] = work[far:, :] - change[far:, :]


def factor_kernel(total_rows, packed_ref, block_ref, basis_ref, upper_ref, one, two, basis, upper, sems):
    row = lax.broadcasted_iota(jnp.int32, (HALF, HALF), 0)
    lane = lax.broadcasted_iota(jnp.int32, (HALF, HALF), 1)
    mixed = packed_ref[:HALF, :] / total_rows
    turned = mixed.T
    diagonal = packed_ref[2 * HALF : 2 * HALF + 1, :] / total_rows
    eye = jnp.where(lane == row, 1.0, 0.0)
    one[:, :HALF] = jnp.where(lane >= row, mixed, turned)
    one[:, HALF : 2 * HALF] = packed_ref[HALF : 2 * HALF, :] / total_rows
    one[:, 2 * HALF :] = eye
    two[:, :HALF] = jnp.where(lane == row, diagonal, jnp.where(lane < row, mixed, turned))
    two[:, HALF:] = eye
    eliminate(one)
    copies = []

    def send(source, target):
        copies.append(pltpu.make_async_copy(source, target, sems.at[len(copies)]))
        copies[-1].start()

    across = one[:, HALF : 2 * HALF]
    upper[:HALF, :HALF] = jnp.where(lane >= row, one[:, :HALF], 0.0)
    upper[:HALF, HALF:] = across
    upper[HALF:, :HALF] = jnp.zeros((HALF, HALF), F32)
    send(upper.at[:HALF], upper_ref.at[:HALF])
    two[:, :HALF] = two[:, :HALF] - dot(across, across, 0, 0)
    left = dot(block_ref[:, :HALF], one[:, 2 * HALF :], 1, 1)
    basis[:, :HALF] = left
    send(basis.at[:, :HALF], basis_ref.at[:, :HALF])
    rest = block_ref[:, HALF:] - dot(left, across, 1, 0)
    basis[:, HALF:] = rest
    eliminate(two)
    upper[HALF:, HALF:] = jnp.where(lane >= row, two[:, :HALF], 0.0)
    send(upper.at[HALF:], upper_ref.at[HALF:])
    quarter = block_ref.shape[0] // 4
    for k in range(4):
        at = slice(k * quarter, (k + 1) * quarter)
        basis[at, HALF:] = dot(basis[at, HALF:], two[:, HALF:], 1, 1)
        send(basis.at[at, HALF:], basis_ref.at[at, HALF:])
    for copy in copies:
        copy.wait()


def factor(total_rows, packed, block):
    return pl.pallas_call(
        functools.partial(factor_kernel, float(total_rows)),
        out_shape=(
            jax.ShapeDtypeStruct(block.shape, F32),
            jax.ShapeDtypeStruct((2 * HALF, 2 * HALF), F32),
        ),
        in_specs=[VMEM] * 2,
        out_specs=(HBM, HBM),
        scratch_shapes=[
            pltpu.VMEM((HALF, 3 * HALF), F32),
            pltpu.VMEM((HALF, 2 * HALF), F32),
            pltpu.VMEM(block.shape, F32),
            pltpu.VMEM((2 * HALF, 2 * HALF), F32),
            pltpu.SemaphoreType.DMA((7,)),
        ],
        compiler_params=SMALL,
        name="factor",
    )(packed, block)


def exchanged(x, axis):
    return lax.all_to_all(x, axis, 0, 0, tiled=True)


def reduced(packed):
    owners, sharers = lax.axis_size(SCATTER), lax.axis_size(SHARED)
    pieces = packed.reshape(owners, 1, -1)
    mine = jnp.sum(exchanged(pieces, SCATTER), axis=0, keepdims=True)
    mine = jnp.broadcast_to(mine, (sharers, *mine.shape[1:]))
    mine = jnp.sum(exchanged(mine, SHARED), axis=0, keepdims=True)
    mine = jnp.broadcast_to(mine, (owners, *mine.shape[1:]))
    return exchanged(mine, SCATTER).reshape(packed.shape)


def local(panel, sketch):
    total_rows = panel.shape[0] * lax.axis_size(ROW)
    core = lax.axis_index("col").astype(jnp.int32).reshape(1)
    other = product(1 - core, panel, sketch)
    came = lax.ppermute(other, "col", [(0, 1), (1, 0)])
    own = product(core, panel, sketch)
    block, packed = gram_of(own, came)
    return factor(total_rows, reduced(packed), block)


def solution(mesh):
    sizes = (4, 2, 4, 2, 4, mesh.shape["col"])
    finer = Mesh(mesh.devices.reshape(sizes), ROW_COL)
    in_specs = (P(ROW, "col"), P("col", None))
    out_specs = (P(ROW_COL, None), P())
    return jax.shard_map(local, mesh=finer, in_specs=in_specs, out_specs=out_specs, check_vma=False)
```

```python
import functools

import jax
import jax.numpy as jnp
from jax import lax
from jax.experimental import pallas as pl
from jax.experimental.pallas import tpu as pltpu
from jax.sharding import Mesh
from jax.sharding import PartitionSpec as P

ROW = ("z_hi", "z_lo", "y_hi", "y_lo", "x")
ROW_COL = (*ROW, "col")
SCATTER = ("z_lo", "y_lo", "x", "col")
SHARED = ("z_hi", "y_hi")
F32 = jnp.float32
BF16 = jnp.bfloat16
VMEM = pl.BlockSpec(memory_space=pltpu.VMEM)
HBM = pl.BlockSpec(memory_space=pltpu.HBM)
HALF = 128
PACKED = 288
SMEM = pl.BlockSpec(memory_space=pltpu.SMEM)
SMALL = pltpu.CompilerParams(vmem_limit_bytes=16 << 20)
CHUNKS = 4


def pieces(x):
    high = x.astype(BF16)
    rest = x - high.astype(F32)
    middle = rest.astype(BF16)
    return high, middle, (rest - middle.astype(F32)).astype(BF16)


def joined(x, dim, order):
    parts = pieces(x)
    return jnp.concatenate([parts[n] for n in order], axis=dim)


LEFT, RIGHT = (0, 0, 0, 1, 1, 2), (0, 1, 2, 0, 1, 0)


def bf16_dot(a, b, dim_a, dim_b):
    dims = (((dim_a,), (dim_b,)), ((), ()))
    return lax.dot_general(a, b, dims, preferred_element_type=F32)


def dot(a, b, dim_a, dim_b):
    return bf16_dot(joined(a, dim_a, LEFT), joined(b, dim_b, RIGHT), dim_a, dim_b)


def other_kernel(core_ref, panel_ref, sketch_ref, out_ref, table_ref, ahead_ref, rows, sems):
    half, depth = rows.shape
    mine = pl.multiple_of(core_ref[0] * half, half)
    other = pl.multiple_of((1 - core_ref[0]) * half, half)
    width = depth // CHUNKS
    copies = []

    def fetch(source, target):
        copies.append(pltpu.make_async_copy(source, target, sems.at[len(copies)]))
        copies[-1].start()

    for k in range(CHUNKS):
        at = slice(k * width, (k + 1) * width)
        fetch(sketch_ref.at[at, :], table_ref.at[at, :])
        fetch(panel_ref.at[pl.ds(other, half), at], rows.at[:, at])
    fetch(panel_ref.at[pl.ds(mine, ahead_ref.shape[0]), :], ahead_ref)
    for k in range(CHUNKS):
        at = slice(k * width, (k + 1) * width)
        copies[2 * k].wait()
        copies[2 * k + 1].wait()
        part = jnp.dot(rows[:, at], table_ref[at, :], preferred_element_type=F32)
        out_ref[...] = part if k == 0 else out_ref[...] + part
    copies[-1].wait()


def own_kernel(core_ref, panel_ref, table_ref, ahead_ref, out_ref, rows, sem):
    early, late = ahead_ref.shape[0], rows.shape[0]
    start = pl.multiple_of(core_ref[0] * (early + late) + early, early)
    copy = pltpu.make_async_copy(panel_ref.at[pl.ds(start, late), :], rows, sem)
    copy.start()
    out_ref[:early, :] = jnp.dot(ahead_ref[...], table_ref[...], preferred_element_type=F32)
    copy.wait()
    out_ref[early:, :] = jnp.dot(rows[...], table_ref[...], preferred_element_type=F32)


def in_hbm(x):
    return pltpu.with_memory_space_constraint(x, pltpu.HBM)


def cost(rows, depth, columns, fetched):
    return pl.CostEstimate(
        flops=2 * rows * depth * columns,
        bytes_accessed=2 * fetched * depth + 4 * rows * columns,
        transcendentals=0,
    )


def other_product(core, panel, sketch):
    rows, depth = panel.shape
    columns = sketch.shape[1]
    half, ahead = rows // 2, rows // 4
    return pl.pallas_call(
        other_kernel,
        out_shape=(
            jax.ShapeDtypeStruct((half, columns), F32),
            jax.ShapeDtypeStruct(sketch.shape, sketch.dtype),
            jax.ShapeDtypeStruct((ahead, depth), panel.dtype),
        ),
        in_specs=[SMEM, HBM, HBM],
        out_specs=(VMEM, VMEM, VMEM),
        scratch_shapes=[
            pltpu.VMEM((half, depth), panel.dtype),
            pltpu.SemaphoreType.DMA((2 * CHUNKS + 1,)),
        ],
        cost_estimate=cost(half, depth, columns, half + ahead + columns),
        compiler_params=SMALL,
        name="other_product",
    )(core, in_hbm(panel), in_hbm(sketch))


def own_product(core, panel, table, ahead):
    depth, columns = table.shape
    half = panel.shape[0] // 2
    late = half - ahead.shape[0]
    return pl.pallas_call(
        own_kernel,
        out_shape=jax.ShapeDtypeStruct((half, columns), F32),
        in_specs=[SMEM, HBM, VMEM, VMEM],
        out_specs=VMEM,
        scratch_shapes=[pltpu.VMEM((late, depth), panel.dtype), pltpu.SemaphoreType.DMA],
        cost_estimate=cost(half, depth, columns, late),
        compiler_params=SMALL,
        name="own_product",
    )(core, in_hbm(panel), table, ahead)


def gram_kernel(own_ref, came_ref, block_ref, packed_ref):
    whole = own_ref[...] + came_ref[...]
    block_ref[...] = whole
    left, right = joined(whole, 0, LEFT), joined(whole, 0, RIGHT)
    top = bf16_dot(left[:, :HALF], right, 0, 0)
    first = top[:, :HALF]
    packed_ref[HALF : 2 * HALF, :] = top[:, HALF:]
    last = bf16_dot(left[:, HALF:], right[:, HALF:], 0, 0)
    row = lax.broadcasted_iota(jnp.int32, (HALF, HALF), 0)
    lane = lax.broadcasted_iota(jnp.int32, (HALF, HALF), 1)
    packed_ref[:HALF, :] = jnp.where(lane >= row, first, last)
    diagonal = jnp.sum(jnp.where(lane == row, last, 0.0), axis=0, keepdims=True)
    packed_ref[2 * HALF :, :] = jnp.broadcast_to(diagonal, (PACKED - 2 * HALF, HALF))


def gram_of(own, came):
    return pl.pallas_call(
        gram_kernel,
        out_shape=(
            jax.ShapeDtypeStruct(own.shape, F32),
            jax.ShapeDtypeStruct((PACKED, HALF), F32),
        ),
        in_specs=[VMEM] * 2,
        out_specs=(VMEM, VMEM),
        compiler_params=SMALL,
        name="gram",
    )(own, came)


def sub(x, j):
    return jnp.broadcast_to(x[j : j + 1, :], (8, HALF))


def lane_of(x, j):
    return jnp.broadcast_to(x[:, j : j + 1], (8, HALF))


def eliminate(work):
    sublane = lax.broadcasted_iota(jnp.int32, (8, HALF), 0)
    size, width = work.shape
    tiles = [slice(t, t + HALF) for t in range(0, width, HALF)]
    block = 16
    for first in range(0, size, block):
        count = min(4, (size - first) // 8)
        rows = [[work[first + 8 * g : first + 8 * g + 8, t] for t in tiles] for g in range(count)]
        cols = [
            [lane_of(rows[g][0], first + m) for m in range(block)]
            for g in range(count)
        ]
        for g in range(2):
            cols[g][0] = jnp.where(sublane < 8, cols[g][0], 0.0)
        pivots = [None, None]
        for j in range(block):
            home, at = divmod(j, 8)
            pivot = sub(cols[home][j], at)
            pivots[home] = pivot if at == 0 else jnp.where(sublane == at, pivot, pivots[home])
            inverse = 1.0 / pivot
            units = [cols[g][j] * inverse for g in range(count)]
            for m in range(j + 1, block):
                spread = sub(cols[m // 8][j], m % 8)
                for g in range(home, count):
                    if g < 2 and m >= 8 * (g + 1):
                        continue
                    cols[g][m] = cols[g][m] - units[g] * spread
            units[home] = jnp.where(sublane > at, units[home], 0.0)
            for t in range(len(tiles)):
                spread = sub(rows[home][t], at)
                for g in range(home, count):
                    rows[g][t] = rows[g][t] - units[g] * spread
        for g in range(count):
            scale = lax.rsqrt(pivots[g]) if g < 2 else None
            for t, tile in enumerate(tiles):
                x = rows[g][t] if scale is None else rows[g][t] * scale
                work[first + 8 * g : first + 8 * g + 8, tile] = x
        far = first + 2 * block
        if far < size:
            done = work[first : first + block, :]
            change = dot(done[:, :HALF], done, 0, 0)
            work[far:, :] = work[far:, :] - change[far:, :]


def factor_kernel(total_rows, packed_ref, block_ref, basis_ref, upper_ref, one, two, basis, upper, sems):
    row = lax.broadcasted_iota(jnp.int32, (HALF, HALF), 0)
    lane = lax.broadcasted_iota(jnp.int32, (HALF, HALF), 1)
    mixed = packed_ref[:HALF, :] / total_rows
    turned = mixed.T
    diagonal = packed_ref[2 * HALF : 2 * HALF + 1, :] / total_rows
    eye = jnp.where(lane == row, 1.0, 0.0)
    one[:, :HALF] = jnp.where(lane >= row, mixed, turned)
    one[:, HALF : 2 * HALF] = packed_ref[HALF : 2 * HALF, :] / total_rows
    one[:, 2 * HALF :] = eye
    two[:, :HALF] = jnp.where(lane == row, diagonal, jnp.where(lane < row, mixed, turned))
    two[:, HALF:] = eye
    eliminate(one)
    copies = []

    def send(source, target):
        copies.append(pltpu.make_async_copy(source, target, sems.at[len(copies)]))
        copies[-1].start()

    across = one[:, HALF : 2 * HALF]
    upper[:HALF, :HALF] = jnp.where(lane >= row, one[:, :HALF], 0.0)
    upper[:HALF, HALF:] = across
    upper[HALF:, :HALF] = jnp.zeros((HALF, HALF), F32)
    send(upper.at[:HALF], upper_ref.at[:HALF])
    two[:, :HALF] = two[:, :HALF] - dot(across, across, 0, 0)
    left = dot(block_ref[:, :HALF], one[:, 2 * HALF :], 1, 1)
    basis[:, :HALF] = left
    send(basis.at[:, :HALF], basis_ref.at[:, :HALF])
    rest = block_ref[:, HALF:] - dot(left, across, 1, 0)
    basis[:, HALF:] = rest
    eliminate(two)
    upper[HALF:, HALF:] = jnp.where(lane >= row, two[:, :HALF], 0.0)
    send(upper.at[HALF:], upper_ref.at[HALF:])
    quarter = block_ref.shape[0] // 4
    for k in range(4):
        at = slice(k * quarter, (k + 1) * quarter)
        basis[at, HALF:] = dot(basis[at, HALF:], two[:, HALF:], 1, 1)
        send(basis.at[at, HALF:], basis_ref.at[at, HALF:])
    for copy in copies:
        copy.wait()


def factor(total_rows, packed, block):
    return pl.pallas_call(
        functools.partial(factor_kernel, float(total_rows)),
        out_shape=(
            jax.ShapeDtypeStruct(block.shape, F32),
            jax.ShapeDtypeStruct((2 * HALF, 2 * HALF), F32),
        ),
        in_specs=[VMEM] * 2,
        out_specs=(HBM, HBM),
        scratch_shapes=[
            pltpu.VMEM((HALF, 3 * HALF), F32),
            pltpu.VMEM((HALF, 2 * HALF), F32),
            pltpu.VMEM(block.shape, F32),
            pltpu.VMEM((2 * HALF, 2 * HALF), F32),
            pltpu.SemaphoreType.DMA((7,)),
        ],
        compiler_params=SMALL,
        name="factor",
    )(packed, block)


def exchanged(x, axis):
    return lax.all_to_all(x, axis, 0, 0, tiled=True)


def reduced(packed):
    owners, sharers = lax.axis_size(SCATTER), lax.axis_size(SHARED)
    pieces = packed.reshape(owners, 1, -1)
    mine = jnp.sum(exchanged(pieces, SCATTER), axis=0, keepdims=True)
    mine = jnp.broadcast_to(mine, (sharers, *mine.shape[1:]))
    mine = jnp.sum(exchanged(mine, SHARED), axis=0, keepdims=True)
    mine = jnp.broadcast_to(mine, (owners, *mine.shape[1:]))
    return exchanged(mine, SCATTER).reshape(packed.shape)


def local(panel, sketch):
    total_rows = panel.shape[0] * lax.axis_size(ROW)
    core = lax.axis_index("col").astype(jnp.int32).reshape(1)
    other, table, ahead = other_product(core, panel, sketch)
    came = lax.ppermute(other, "col", [(0, 1), (1, 0)])
    own = own_product(core, panel, table, ahead)
    block, packed = gram_of(own, came)
    return factor(total_rows, reduced(packed), block)


def solution(mesh):
    sizes = (4, 2, 4, 2, 4, mesh.shape["col"])
    finer = Mesh(mesh.devices.reshape(sizes), ROW_COL)
    in_specs = (P(ROW, "col"), P("col", None))
    out_specs = (P(ROW_COL, None), P())
    return jax.shard_map(local, mesh=finer, in_specs=in_specs, out_specs=out_specs, check_vma=False)
```

```python
import functools

import jax
import jax.numpy as jnp
from jax import lax
from jax.experimental import pallas as pl
from jax.experimental.pallas import tpu as pltpu
from jax.sharding import Mesh
from jax.sharding import PartitionSpec as P

ROW = ("z_hi", "z_lo", "y_hi", "y_lo", "x")
ROW_COL = (*ROW, "col")
SCATTER = ("z_lo", "y_lo", "x", "col")
SHARED = ("z_hi", "z_lo", "y_hi", "y_lo")
F32 = jnp.float32
BF16 = jnp.bfloat16
VMEM = pl.BlockSpec(memory_space=pltpu.VMEM)
HBM = pl.BlockSpec(memory_space=pltpu.HBM)
HALF = 128
PACKED = 288
QUARTERS = 4
SMEM = pl.BlockSpec(memory_space=pltpu.SMEM)
SMALL = pltpu.CompilerParams(vmem_limit_bytes=16 << 20)
CHUNKS = 4


def pieces(x):
    high = x.astype(BF16)
    rest = x - high.astype(F32)
    middle = rest.astype(BF16)
    return high, middle, (rest - middle.astype(F32)).astype(BF16)


def joined(x, dim, order):
    parts = pieces(x)
    return jnp.concatenate([parts[n] for n in order], axis=dim)


LEFT, RIGHT = (0, 0, 0, 1, 1, 2), (0, 1, 2, 0, 1, 0)


def bf16_dot(a, b, dim_a, dim_b):
    dims = (((dim_a,), (dim_b,)), ((), ()))
    return lax.dot_general(a, b, dims, preferred_element_type=F32)


def dot(a, b, dim_a, dim_b):
    return bf16_dot(joined(a, dim_a, LEFT), joined(b, dim_b, RIGHT), dim_a, dim_b)


def other_kernel(core_ref, panel_ref, sketch_ref, out_ref, table_ref, ahead_ref, rows, sems):
    half, depth = rows.shape
    mine = pl.multiple_of(core_ref[0] * half, half)
    other = pl.multiple_of((1 - core_ref[0]) * half, half)
    width = depth // CHUNKS
    copies = []

    def fetch(source, target):
        copies.append(pltpu.make_async_copy(source, target, sems.at[len(copies)]))
        copies[-1].start()

    for k in range(CHUNKS):
        at = slice(k * width, (k + 1) * width)
        fetch(sketch_ref.at[at, :], table_ref.at[at, :])
        fetch(panel_ref.at[pl.ds(other, half), at], rows.at[:, at])
    fetch(panel_ref.at[pl.ds(mine, ahead_ref.shape[0]), :], ahead_ref)
    for k in range(CHUNKS):
        at = slice(k * width, (k + 1) * width)
        copies[2 * k].wait()
        copies[2 * k + 1].wait()
        part = jnp.dot(rows[:, at], table_ref[at, :], preferred_element_type=F32)
        out_ref[...] = part if k == 0 else out_ref[...] + part
    copies[-1].wait()


def own_kernel(core_ref, panel_ref, table_ref, ahead_ref, out_ref, rows, sem):
    early, late = ahead_ref.shape[0], rows.shape[0]
    start = pl.multiple_of(core_ref[0] * (early + late) + early, early)
    copy = pltpu.make_async_copy(panel_ref.at[pl.ds(start, late), :], rows, sem)
    copy.start()
    out_ref[:early, :] = jnp.dot(ahead_ref[...], table_ref[...], preferred_element_type=F32)
    copy.wait()
    out_ref[early:, :] = jnp.dot(rows[...], table_ref[...], preferred_element_type=F32)


def in_hbm(x):
    return pltpu.with_memory_space_constraint(x, pltpu.HBM)


def cost(rows, depth, columns, fetched):
    return pl.CostEstimate(
        flops=2 * rows * depth * columns,
        bytes_accessed=2 * fetched * depth + 4 * rows * columns,
        transcendentals=0,
    )


def other_product(core, panel, sketch):
    rows, depth = panel.shape
    columns = sketch.shape[1]
    half, ahead = rows // 2, rows // 4
    return pl.pallas_call(
        other_kernel,
        out_shape=(
            jax.ShapeDtypeStruct((half, columns), F32),
            jax.ShapeDtypeStruct(sketch.shape, sketch.dtype),
            jax.ShapeDtypeStruct((ahead, depth), panel.dtype),
        ),
        in_specs=[SMEM, HBM, HBM],
        out_specs=(VMEM, VMEM, VMEM),
        scratch_shapes=[
            pltpu.VMEM((half, depth), panel.dtype),
            pltpu.SemaphoreType.DMA((2 * CHUNKS + 1,)),
        ],
        cost_estimate=cost(half, depth, columns, half + ahead + columns),
        compiler_params=SMALL,
        name="other_product",
    )(core, in_hbm(panel), in_hbm(sketch))


def own_product(core, panel, table, ahead):
    depth, columns = table.shape
    half = panel.shape[0] // 2
    late = half - ahead.shape[0]
    return pl.pallas_call(
        own_kernel,
        out_shape=jax.ShapeDtypeStruct((half, columns), F32),
        in_specs=[SMEM, HBM, VMEM, VMEM],
        out_specs=VMEM,
        scratch_shapes=[pltpu.VMEM((late, depth), panel.dtype), pltpu.SemaphoreType.DMA],
        cost_estimate=cost(half, depth, columns, late),
        compiler_params=SMALL,
        name="own_product",
    )(core, in_hbm(panel), table, ahead)


def gram_kernel(turn_ref, own_ref, came_ref, block_ref, placed_ref, packed_ref):
    whole = own_ref[...] + came_ref[...]
    block_ref[...] = whole
    left, right = joined(whole, 0, LEFT), joined(whole, 0, RIGHT)
    top = bf16_dot(left[:, :HALF], right, 0, 0)
    first = top[:, :HALF]
    packed_ref[HALF : 2 * HALF, :] = top[:, HALF:]
    last = bf16_dot(left[:, HALF:], right[:, HALF:], 0, 0)
    row = lax.broadcasted_iota(jnp.int32, (HALF, HALF), 0)
    lane = lax.broadcasted_iota(jnp.int32, (HALF, HALF), 1)
    packed_ref[:HALF, :] = jnp.where(lane >= row, first, last)
    diagonal = jnp.sum(jnp.where(lane == row, last, 0.0), axis=0, keepdims=True)
    packed_ref[2 * HALF :, :] = jnp.broadcast_to(diagonal, (PACKED - 2 * HALF, HALF))
    for k in range(QUARTERS):
        placed_ref[owners_place(turn_ref, k), :] = packed_ref[quarter(k), :]


def quarter(k):
    return slice(k * PACKED // QUARTERS, (k + 1) * PACKED // QUARTERS)


def owners_place(turn_ref, k):
    rows = PACKED // QUARTERS
    return pl.ds(pl.multiple_of((k ^ turn_ref[0]) * rows, 8), rows)


def gram_of(turn, own, came):
    return pl.pallas_call(
        gram_kernel,
        out_shape=(
            jax.ShapeDtypeStruct(own.shape, F32),
            jax.ShapeDtypeStruct((PACKED, HALF), F32),
        ),
        in_specs=[SMEM, VMEM, VMEM],
        out_specs=(VMEM, VMEM),
        scratch_shapes=[pltpu.VMEM((PACKED, HALF), F32)],
        compiler_params=SMALL,
        name="gram",
    )(turn, own, came)


def sub(x, j):
    return jnp.broadcast_to(x[j : j + 1, :], (8, HALF))


def lane_of(x, j):
    return jnp.broadcast_to(x[:, j : j + 1], (8, HALF))


def eliminate(work):
    sublane = lax.broadcasted_iota(jnp.int32, (8, HALF), 0)
    size, width = work.shape
    tiles = [slice(t, t + HALF) for t in range(0, width, HALF)]
    block = 16
    for first in range(0, size, block):
        left = (size - first - block) // 8
        look = left if left <= 4 else 3
        count = 2 + look
        rows = [[work[first + 8 * g : first + 8 * g + 8, t] for t in tiles] for g in range(count)]
        cols = [
            [lane_of(rows[g][0], first + m) for m in range(block)]
            for g in range(count)
        ]
        for g in range(2):
            cols[g][0] = jnp.where(sublane < 8, cols[g][0], 0.0)
        pivots = [None, None]
        for j in range(block):
            home, at = divmod(j, 8)
            pivot = sub(cols[home][j], at)
            pivots[home] = pivot if at == 0 else jnp.where(sublane == at, pivot, pivots[home])
            inverse = 1.0 / pivot
            units = [cols[g][j] * inverse for g in range(count)]
            for m in range(j + 1, block):
                spread = sub(cols[m // 8][j], m % 8)
                for g in range(home, count):
                    if g < 2 and m >= 8 * (g + 1):
                        continue
                    cols[g][m] = cols[g][m] - units[g] * spread
            units[home] = jnp.where(sublane > at, units[home], 0.0)
            for t in range(len(tiles)):
                spread = sub(rows[home][t], at)
                for g in range(home, count):
                    rows[g][t] = rows[g][t] - units[g] * spread
        for g in range(count):
            scale = lax.rsqrt(pivots[g]) if g < 2 else None
            for t, tile in enumerate(tiles):
                x = rows[g][t] if scale is None else rows[g][t] * scale
                work[first + 8 * g : first + 8 * g + 8, tile] = x
        far = first + block + 8 * look
        if far < size:
            done = work[first : first + block, :]
            change = dot(done[:, :HALF], done, 0, 0)
            work[far:, :] = work[far:, :] - change[far:, :]


def factor_kernel(
    total_rows, turn_ref, placed_ref, block_ref, basis_ref, upper_ref, packed_ref, one, two, basis, upper, sems
):
    for k in range(QUARTERS):
        packed_ref[quarter(k), :] = placed_ref[owners_place(turn_ref, k), :]
    row = lax.broadcasted_iota(jnp.int32, (HALF, HALF), 0)
    lane = lax.broadcasted_iota(jnp.int32, (HALF, HALF), 1)
    mixed = packed_ref[:HALF, :] / total_rows
    turned = mixed.T
    diagonal = packed_ref[2 * HALF : 2 * HALF + 1, :] / total_rows
    eye = jnp.where(lane == row, 1.0, 0.0)
    one[:, :HALF] = jnp.where(lane >= row, mixed, turned)
    one[:, HALF : 2 * HALF] = packed_ref[HALF : 2 * HALF, :] / total_rows
    one[:, 2 * HALF :] = eye
    two[:, :HALF] = jnp.where(lane == row, diagonal, jnp.where(lane < row, mixed, turned))
    two[:, HALF:] = eye
    eliminate(one)
    copies = []

    def send(source, target):
        copies.append(pltpu.make_async_copy(source, target, sems.at[len(copies)]))
        copies[-1].start()

    across = one[:, HALF : 2 * HALF]
    upper[:HALF, :HALF] = jnp.where(lane >= row, one[:, :HALF], 0.0)
    upper[:HALF, HALF:] = across
    upper[HALF:, :HALF] = jnp.zeros((HALF, HALF), F32)
    send(upper.at[:HALF], upper_ref.at[:HALF])
    two[:, :HALF] = two[:, :HALF] - dot(across, across, 0, 0)
    left = dot(block_ref[:, :HALF], one[:, 2 * HALF :], 1, 1)
    basis[:, :HALF] = left
    send(basis.at[:, :HALF], basis_ref.at[:, :HALF])
    rest = block_ref[:, HALF:] - dot(left, across, 1, 0)
    basis[:, HALF:] = rest
    eliminate(two)
    upper[HALF:, HALF:] = jnp.where(lane >= row, two[:, :HALF], 0.0)
    send(upper.at[HALF:], upper_ref.at[HALF:])
    strip = block_ref.shape[0] // 4
    for k in range(4):
        at = slice(k * strip, (k + 1) * strip)
        basis[at, HALF:] = dot(basis[at, HALF:], two[:, HALF:], 1, 1)
        send(basis.at[at, HALF:], basis_ref.at[at, HALF:])
    for copy in copies:
        copy.wait()


def factor(total_rows, turn, placed, block):
    return pl.pallas_call(
        functools.partial(factor_kernel, float(total_rows)),
        out_shape=(
            jax.ShapeDtypeStruct(block.shape, F32),
            jax.ShapeDtypeStruct((2 * HALF, 2 * HALF), F32),
        ),
        in_specs=[SMEM, VMEM, VMEM],
        out_specs=(HBM, HBM),
        scratch_shapes=[
            pltpu.VMEM((PACKED, HALF), F32),
            pltpu.VMEM((HALF, 3 * HALF), F32),
            pltpu.VMEM((HALF, 2 * HALF), F32),
            pltpu.VMEM(block.shape, F32),
            pltpu.VMEM((2 * HALF, 2 * HALF), F32),
            pltpu.SemaphoreType.DMA((7,)),
        ],
        compiler_params=SMALL,
        name="factor",
    )(turn, placed, block)


def turned(high):
    return 1 - (((high + 1) >> 1) & 1)


def sharers():
    z_pairs, y_pairs = lax.axis_size("z_hi"), lax.axis_size("y_hi")
    return [
        [
            ((z * 2 + (i ^ turned(z))) * y_pairs + y) * 2 + (j ^ turned(y))
            for z in range(z_pairs)
            for y in range(y_pairs)
        ]
        for i in range(2)
        for j in range(2)
    ]


def exchanged(x, axis, groups=None):
    return lax.all_to_all(x, axis, 0, 0, axis_index_groups=groups, tiled=True)


def reduced(placed):
    owners, groups = lax.axis_size(SCATTER), sharers()
    pieces = placed.reshape(owners, 1, -1)
    mine = jnp.sum(exchanged(pieces, SCATTER), axis=0, keepdims=True)
    mine = jnp.broadcast_to(mine, (len(groups[0]), *mine.shape[1:]))
    mine = jnp.sum(exchanged(mine, SHARED, groups), axis=0, keepdims=True)
    mine = jnp.broadcast_to(mine, (owners, *mine.shape[1:]))
    return exchanged(mine, SCATTER).reshape(placed.shape)


def local(panel, sketch):
    total_rows = panel.shape[0] * lax.axis_size(ROW)
    core = lax.axis_index("col").astype(jnp.int32).reshape(1)
    other, table, ahead = other_product(core, panel, sketch)
    came = lax.ppermute(other, "col", [(0, 1), (1, 0)])
    own = own_product(core, panel, table, ahead)
    turn = 2 * turned(lax.axis_index("z_hi")) + turned(lax.axis_index("y_hi"))
    turn = turn.astype(jnp.int32).reshape(1)
    block, placed = gram_of(turn, own, came)
    return factor(total_rows, turn, reduced(placed), block)


def solution(mesh):
    sizes = (4, 2, 4, 2, 4, mesh.shape["col"])
    finer = Mesh(mesh.devices.reshape(sizes), ROW_COL)
    in_specs = (P(ROW, "col"), P("col", None))
    out_specs = (P(ROW_COL, None), P())
    return jax.shard_map(local, mesh=finer, in_specs=in_specs, out_specs=out_specs, check_vma=False)
```

```python
import functools

import jax
import jax.numpy as jnp
from jax import lax
from jax.experimental import pallas as pl
from jax.experimental.pallas import tpu as pltpu
from jax.sharding import Mesh
from jax.sharding import PartitionSpec as P

ROW = ("z_hi", "z_lo", "y_hi", "y_lo", "x")
ROW_COL = (*ROW, "col")
SCATTER = ("z_lo", "y_lo", "x", "col")
SHARED = ("z_hi", "z_lo", "y_hi", "y_lo")
F32 = jnp.float32
BF16 = jnp.bfloat16
VMEM = pl.BlockSpec(memory_space=pltpu.VMEM)
HBM = pl.BlockSpec(memory_space=pltpu.HBM)
HALF = 128
PACKED = 288
QUARTERS = 4
SMEM = pl.BlockSpec(memory_space=pltpu.SMEM)
SMALL = pltpu.CompilerParams(vmem_limit_bytes=16 << 20)
CHUNKS = (3, 3, 2)


def pieces(x):
    high = x.astype(BF16)
    rest = x - high.astype(F32)
    middle = rest.astype(BF16)
    return high, middle, (rest - middle.astype(F32)).astype(BF16)


def joined(x, dim, order):
    parts = pieces(x)
    return jnp.concatenate([parts[n] for n in order], axis=dim)


LEFT, RIGHT = (0, 0, 0, 1, 1, 2), (0, 1, 2, 0, 1, 0)


def bf16_dot(a, b, dim_a, dim_b):
    dims = (((dim_a,), (dim_b,)), ((), ()))
    return lax.dot_general(a, b, dims, preferred_element_type=F32)


def dot(a, b, dim_a, dim_b):
    return bf16_dot(joined(a, dim_a, LEFT), joined(b, dim_b, RIGHT), dim_a, dim_b)


def other_kernel(core_ref, panel_ref, sketch_ref, out_ref, table_ref, ahead_ref, rows, sems):
    half, depth = rows.shape
    mine = pl.multiple_of(core_ref[0] * half, half)
    other = pl.multiple_of((1 - core_ref[0]) * half, half)
    unit = depth // sum(CHUNKS)
    ends = [unit * sum(CHUNKS[:k]) for k in range(len(CHUNKS) + 1)]
    chunks = [slice(*at) for at in zip(ends, ends[1:])]
    copies = []

    def fetch(source, target):
        copies.append(pltpu.make_async_copy(source, target, sems.at[len(copies)]))
        copies[-1].start()

    for at in chunks:
        fetch(sketch_ref.at[at, :], table_ref.at[at, :])
        fetch(panel_ref.at[pl.ds(other, half), at], rows.at[:, at])
    fetch(panel_ref.at[pl.ds(mine, ahead_ref.shape[0]), :], ahead_ref)
    for k, at in enumerate(chunks):
        copies[2 * k].wait()
        copies[2 * k + 1].wait()
        part = jnp.dot(rows[:, at], table_ref[at, :], preferred_element_type=F32)
        out_ref[...] = part if k == 0 else out_ref[...] + part
    copies[-1].wait()


def own_kernel(core_ref, panel_ref, table_ref, ahead_ref, out_ref, rows, sem):
    early, late = ahead_ref.shape[0], rows.shape[0]
    start = pl.multiple_of(core_ref[0] * (early + late) + early, early)
    copy = pltpu.make_async_copy(panel_ref.at[pl.ds(start, late), :], rows, sem)
    copy.start()
    out_ref[:early, :] = jnp.dot(ahead_ref[...], table_ref[...], preferred_element_type=F32)
    copy.wait()
    out_ref[early:, :] = jnp.dot(rows[...], table_ref[...], preferred_element_type=F32)


def in_hbm(x):
    return pltpu.with_memory_space_constraint(x, pltpu.HBM)


def cost(rows, depth, columns, fetched):
    return pl.CostEstimate(
        flops=2 * rows * depth * columns,
        bytes_accessed=2 * fetched * depth + 4 * rows * columns,
        transcendentals=0,
    )


def other_product(core, panel, sketch):
    rows, depth = panel.shape
    columns = sketch.shape[1]
    half, ahead = rows // 2, rows // 4
    return pl.pallas_call(
        other_kernel,
        out_shape=(
            jax.ShapeDtypeStruct((half, columns), F32),
            jax.ShapeDtypeStruct(sketch.shape, sketch.dtype),
            jax.ShapeDtypeStruct((ahead, depth), panel.dtype),
        ),
        in_specs=[SMEM, HBM, HBM],
        out_specs=(VMEM, VMEM, VMEM),
        scratch_shapes=[
            pltpu.VMEM((half, depth), panel.dtype),
            pltpu.SemaphoreType.DMA((2 * len(CHUNKS) + 1,)),
        ],
        cost_estimate=cost(half, depth, columns, half + ahead + columns),
        compiler_params=SMALL,
        name="other_product",
    )(core, in_hbm(panel), in_hbm(sketch))


def own_product(core, panel, table, ahead):
    depth, columns = table.shape
    half = panel.shape[0] // 2
    late = half - ahead.shape[0]
    return pl.pallas_call(
        own_kernel,
        out_shape=jax.ShapeDtypeStruct((half, columns), F32),
        in_specs=[SMEM, HBM, VMEM, VMEM],
        out_specs=VMEM,
        scratch_shapes=[pltpu.VMEM((late, depth), panel.dtype), pltpu.SemaphoreType.DMA],
        cost_estimate=cost(half, depth, columns, late),
        compiler_params=SMALL,
        name="own_product",
    )(core, in_hbm(panel), table, ahead)


def gram_kernel(turn_ref, own_ref, came_ref, block_ref, placed_ref, packed_ref):
    whole = own_ref[...] + came_ref[...]
    block_ref[...] = whole
    left, right = joined(whole, 0, LEFT), joined(whole, 0, RIGHT)
    top = bf16_dot(left[:, :HALF], right, 0, 0)
    first = top[:, :HALF]
    packed_ref[HALF : 2 * HALF, :] = top[:, HALF:]
    last = bf16_dot(left[:, HALF:], right[:, HALF:], 0, 0)
    row = lax.broadcasted_iota(jnp.int32, (HALF, HALF), 0)
    lane = lax.broadcasted_iota(jnp.int32, (HALF, HALF), 1)
    packed_ref[:HALF, :] = jnp.where(lane >= row, first, last)
    diagonal = jnp.sum(jnp.where(lane == row, last, 0.0), axis=0, keepdims=True)
    packed_ref[2 * HALF :, :] = jnp.broadcast_to(diagonal, (PACKED - 2 * HALF, HALF))
    for k in range(QUARTERS):
        placed_ref[owners_place(turn_ref, k), :] = packed_ref[quarter(k), :]


def quarter(k):
    return slice(k * PACKED // QUARTERS, (k + 1) * PACKED // QUARTERS)


def owners_place(turn_ref, k):
    rows = PACKED // QUARTERS
    return pl.ds(pl.multiple_of((k ^ turn_ref[0]) * rows, 8), rows)


def gram_of(turn, own, came):
    return pl.pallas_call(
        gram_kernel,
        out_shape=(
            jax.ShapeDtypeStruct(own.shape, F32),
            jax.ShapeDtypeStruct((PACKED, HALF), F32),
        ),
        in_specs=[SMEM, VMEM, VMEM],
        out_specs=(VMEM, VMEM),
        scratch_shapes=[pltpu.VMEM((PACKED, HALF), F32)],
        compiler_params=SMALL,
        name="gram",
    )(turn, own, came)


def sub(x, j):
    return jnp.broadcast_to(x[j : j + 1, :], (8, HALF))


def lane_of(x, j):
    return jnp.broadcast_to(x[:, j : j + 1], (8, HALF))


def eliminate(work):
    sublane = lax.broadcasted_iota(jnp.int32, (8, HALF), 0)
    size, width = work.shape
    tiles = [slice(t, t + HALF) for t in range(0, width, HALF)]
    block = 16
    for first in range(0, size, block):
        left = (size - first - block) // 8
        lazy = left > 4
        look = 3 if lazy else left
        count = 2 + look
        rows = [[work[first + 8 * g : first + 8 * g + 8, t] for t in tiles] for g in range(count)]
        cols = [
            [lane_of(rows[g][0], first + m) for m in range(block)]
            for g in range(count)
        ]
        for g in range(2):
            cols[g][0] = jnp.where(sublane < 8, cols[g][0], 0.0)
        pivots = [None, None]
        for j in range(block):
            home, at = divmod(j, 8)
            pivot = sub(cols[home][j], at)
            pivots[home] = pivot if at == 0 else jnp.where(sublane == at, pivot, pivots[home])
            inverse = 1.0 / pivot
            units = [cols[g][j] * inverse for g in range(count)]
            for m in range(j + 1, block):
                spread = sub(cols[m // 8][j], m % 8)
                for g in range(home, count):
                    if g < 2 and m >= 8 * (g + 1):
                        continue
                    cols[g][m] = cols[g][m] - units[g] * spread
            units[home] = jnp.where(sublane > at, units[home], 0.0)
            for t in range(len(tiles)):
                spread = sub(rows[home][t], at)
                for g in range(home, 2 if lazy and t else count):
                    rows[g][t] = rows[g][t] - units[g] * spread
        for g in range(count):
            scale = lax.rsqrt(pivots[g]) if g < 2 else None
            for t, tile in enumerate(tiles):
                if lazy and t and g >= 2:
                    continue
                x = rows[g][t] if scale is None else rows[g][t] * scale
                work[first + 8 * g : first + 8 * g + 8, tile] = x
        if lazy:
            near, far = first + block, first + block + 8 * look
            done = work[first : first + block, :]
            change = dot(done[:, :HALF], done, 0, 0)
            work[far:, :HALF] = work[far:, :HALF] - change[far:, :HALF]
            work[near:, HALF:] = work[near:, HALF:] - change[near:, HALF:]


def factor_kernel(
    total_rows, turn_ref, placed_ref, block_ref, basis_ref, upper_ref, packed_ref, one, two, basis, upper, sems
):
    for k in range(QUARTERS):
        packed_ref[quarter(k), :] = placed_ref[owners_place(turn_ref, k), :]
    row = lax.broadcasted_iota(jnp.int32, (HALF, HALF), 0)
    lane = lax.broadcasted_iota(jnp.int32, (HALF, HALF), 1)
    mixed = packed_ref[:HALF, :] / total_rows
    turned = mixed.T
    diagonal = packed_ref[2 * HALF : 2 * HALF + 1, :] / total_rows
    eye = jnp.where(lane == row, 1.0, 0.0)
    one[:, :HALF] = jnp.where(lane >= row, mixed, turned)
    one[:, HALF : 2 * HALF] = packed_ref[HALF : 2 * HALF, :] / total_rows
    one[:, 2 * HALF :] = eye
    two[:, :HALF] = jnp.where(lane == row, diagonal, jnp.where(lane < row, mixed, turned))
    two[:, HALF:] = eye
    eliminate(one)
    copies = []

    def send(source, target):
        copies.append(pltpu.make_async_copy(source, target, sems.at[len(copies)]))
        copies[-1].start()

    across = one[:, HALF : 2 * HALF]
    upper[:HALF, :HALF] = jnp.where(lane >= row, one[:, :HALF], 0.0)
    upper[:HALF, HALF:] = across
    upper[HALF:, :HALF] = jnp.zeros((HALF, HALF), F32)
    send(upper.at[:HALF], upper_ref.at[:HALF])
    two[:, :HALF] = two[:, :HALF] - dot(across, across, 0, 0)
    left = dot(block_ref[:, :HALF], one[:, 2 * HALF :], 1, 1)
    basis[:, :HALF] = left
    send(basis.at[:, :HALF], basis_ref.at[:, :HALF])
    rest = block_ref[:, HALF:] - dot(left, across, 1, 0)
    basis[:, HALF:] = rest
    eliminate(two)
    upper[HALF:, HALF:] = jnp.where(lane >= row, two[:, :HALF], 0.0)
    send(upper.at[HALF:], upper_ref.at[HALF:])
    strip = block_ref.shape[0] // 4
    for k in range(4):
        at = slice(k * strip, (k + 1) * strip)
        basis[at, HALF:] = dot(basis[at, HALF:], two[:, HALF:], 1, 1)
        send(basis.at[at, HALF:], basis_ref.at[at, HALF:])
    for copy in copies:
        copy.wait()


def factor(total_rows, turn, placed, block):
    return pl.pallas_call(
        functools.partial(factor_kernel, float(total_rows)),
        out_shape=(
            jax.ShapeDtypeStruct(block.shape, F32),
            jax.ShapeDtypeStruct((2 * HALF, 2 * HALF), F32),
        ),
        in_specs=[SMEM, VMEM, VMEM],
        out_specs=(HBM, HBM),
        scratch_shapes=[
            pltpu.VMEM((PACKED, HALF), F32),
            pltpu.VMEM((HALF, 3 * HALF), F32),
            pltpu.VMEM((HALF, 2 * HALF), F32),
            pltpu.VMEM(block.shape, F32),
            pltpu.VMEM((2 * HALF, 2 * HALF), F32),
            pltpu.SemaphoreType.DMA((7,)),
        ],
        compiler_params=SMALL,
        name="factor",
    )(turn, placed, block)


def turned(high):
    return 1 - (((high + 1) >> 1) & 1)


def sharers():
    z_pairs, y_pairs = lax.axis_size("z_hi"), lax.axis_size("y_hi")
    return [
        [
            ((z * 2 + (i ^ turned(z))) * y_pairs + y) * 2 + (j ^ turned(y))
            for z in range(z_pairs)
            for y in range(y_pairs)
        ]
        for i in range(2)
        for j in range(2)
    ]


def exchanged(x, axis, groups=None):
    return lax.all_to_all(x, axis, 0, 0, axis_index_groups=groups, tiled=True)


def reduced(placed):
    owners, groups = lax.axis_size(SCATTER), sharers()
    pieces = placed.reshape(owners, 1, -1)
    mine = jnp.sum(exchanged(pieces, SCATTER), axis=0, keepdims=True)
    mine = jnp.broadcast_to(mine, (len(groups[0]), *mine.shape[1:]))
    mine = jnp.sum(exchanged(mine, SHARED, groups), axis=0, keepdims=True)
    mine = jnp.broadcast_to(mine, (owners, *mine.shape[1:]))
    return exchanged(mine, SCATTER).reshape(placed.shape)


def local(panel, sketch):
    total_rows = panel.shape[0] * lax.axis_size(ROW)
    core = lax.axis_index("col").astype(jnp.int32).reshape(1)
    other, table, ahead = other_product(core, panel, sketch)
    came = lax.ppermute(other, "col", [(0, 1), (1, 0)])
    own = own_product(core, panel, table, ahead)
    turn = 2 * turned(lax.axis_index("z_hi")) + turned(lax.axis_index("y_hi"))
    turn = turn.astype(jnp.int32).reshape(1)
    block, placed = gram_of(turn, own, came)
    return factor(total_rows, turn, reduced(placed), block)


def solution(mesh):
    sizes = (4, 2, 4, 2, 4, mesh.shape["col"])
    finer = Mesh(mesh.devices.reshape(sizes), ROW_COL)
    in_specs = (P(ROW, "col"), P("col", None))
    out_specs = (P(ROW_COL, None), P())
    return jax.shard_map(local, mesh=finer, in_specs=in_specs, out_specs=out_specs, check_vma=False)
```
